32 devices in a mesh: tm: 8 (over y, x, core), op: 4 (over z).
Axes of the slice: x: 2, y: 2, z: 4, core: 2. Of those that a mesh axis runs over, the one named last changes fastest.
Arguments:
- perambs: float32 [8, 8, 2, 256, 256], P('tm'), may hold values from -0.25 to 0.25
- src_ops: float32 [4, 8, 2, 256, 256], P('op', 'tm'), may hold values from -0.25 to 0.25
- sink_ops: float32 [4, 8, 2, 256, 256], P('op', 'tm'), may hold values from -0.25 to 0.25
- pair_list: int32 [4, 4], P('op'), may hold values from 0 to 3
- pair_count: int32 [4], P('op'), may hold values from 1 to 4, as said below
Outputs:
- corr: float32 [4, 4, 8, 2, 8], P('op', None, 'tm')
The draws below stay inside these ranges and needn't reach their ends.
Inputs may be any that keep to these rules, and one draw needn't show every extreme that they name: The owner of operator a has pair_count[a] diagrams in slots 0 to pair_count[a] - 1; later slots hold no diagram. Some operator has all 4 slots filled in every draw.
All inputs are finite; a program needn't handle non-finite values.
Results may differ from the reference program's by a relative error of at most 0.0003.
Values sent between devices are 32-bit elements; how exact they have to be, the bound alone decides.
A program may use at most 64 MiB of HBM per device.

```python
import jax
import jax.numpy as jnp
from jax import lax

ORDER = 256
SLOTS = 4
T_SIZE = 8
OPS = 4


def draw_pair_count(key, part):
    first, second = jax.random.split(jax.random.fold_in(key, 11))
    counts = jax.random.randint(first, (OPS,), 1, SLOTS + 1)
    fullest = jax.random.randint(second, (), 0, OPS)
    return jnp.where(jnp.arange(OPS) == fullest, SLOTS, counts).astype(jnp.int32)


def with_ends(entries, rng, least, high):
    index_at = [jax.random.randint(jax.random.fold_in(rng, axis), (), 0, length) for axis, length in enumerate(entries.shape)]
    main_axis = entries.shape.index(max(entries.shape))
    neighbour = index_at[:main_axis] + [(index_at[main_axis] + 1) % entries.shape[main_axis]] + index_at[main_axis + 1:]
    return entries.at[tuple(index_at)].set(least).at[tuple(neighbour)].set(high)


def steps_of(key, extent, cuts, low, largest):
    gain, own = 1.0, jax.random.fold_in(key, 6)
    for dim, blocks in cuts:
        steps = jnp.exp(jax.random.uniform(jax.random.fold_in(own, dim), (blocks,), jnp.float32, low / len(cuts), largest / len(cuts)))
        gain = gain * jnp.repeat(steps, extent[dim] // blocks).reshape([-1 if axis == dim else 1 for axis in range(len(extent))])
    return gain


def noise(rng, dims, spread, most, pieces=(), kind=jnp.bfloat16):
    array = spread * jax.random.normal(rng, dims, jnp.float32)
    if pieces:
        array = array * steps_of(rng, dims, pieces, -0.22, 0.18)
    return jnp.clip(array, -most, most).astype(kind)


def setup_inputs(seed: int = 0) -> dict:
    key_of = jax.random.split(jax.random.key(seed), 6)
    perambs = noise(key_of[0], (T_SIZE, T_SIZE, 2, ORDER, ORDER), (2 * ORDER) ** -0.5, 0.25, ((0, 8),), jnp.float32)
    src_ops = noise(key_of[1], (OPS, T_SIZE, 2, ORDER, ORDER), (2 * ORDER) ** -0.5, 0.25, ((0, 4), (1, 8)), jnp.float32)
    sink_ops = noise(key_of[2], (OPS, T_SIZE, 2, ORDER, ORDER), (2 * ORDER) ** -0.5, 0.25, ((0, 4), (1, 8)), jnp.float32)
    pair_list = with_ends(jax.random.randint(key_of[3], (OPS, SLOTS), 0, OPS), jax.random.fold_in(key_of[3], 1), 0, OPS - 1).astype(jnp.int32)
    pair_count = draw_pair_count(jax.random.fold_in(key_of[5], 71), 0)
    return dict(perambs=perambs, src_ops=src_ops, sink_ops=sink_ops, pair_list=pair_list, pair_count=pair_count)


highest = lax.Precision.HIGHEST


def complex_product(left_re, left_im, right_re, right_im):
    real_part = jnp.matmul(left_re, right_re, precision=highest) - jnp.matmul(left_im, right_im, precision=highest)
    imag_part = jnp.matmul(left_re, right_im, precision=highest) + jnp.matmul(left_im, right_re, precision=highest)
    return real_part, imag_part


def reference(perambs, src_ops, sink_ops, pair_list, pair_count):
    slot_index = jnp.arange(SLOTS).astype(jnp.int32)

    def one_owner(owner):
        source = src_ops[owner]
        listing = pair_list[owner]
        live = (slot_index < pair_count[owner]).astype(jnp.float32)

        def one_sink(sink):
            peramb = perambs[sink]
            chosen = jnp.take(sink_ops[:, sink], listing, axis=0)
            half_re, half_im = complex_product(peramb[:, 0], peramb[:, 1], source[:, 0], source[:, 1])
            prod_re, prod_im = complex_product(half_re, half_im, jnp.swapaxes(peramb[:, 0], 1, 2), -jnp.swapaxes(peramb[:, 1], 1, 2))
            pair_re, pair_im = complex_product(prod_re[:, None], prod_im[:, None], chosen[None, :, 0], chosen[None, :, 1])
            swap_re = jnp.swapaxes(pair_re, 2, 3)
            swap_im = jnp.swapaxes(pair_im, 2, 3)
            trace_re = jnp.sum(pair_re * swap_re, axis=(2, 3)) - jnp.sum(pair_im * swap_im, axis=(2, 3))
            trace_im = 2.0 * jnp.sum(pair_re * swap_im, axis=(2, 3))
            values = jnp.stack([trace_re, trace_im], axis=0)
            values = jnp.transpose(values, (2, 0, 1))
            return values * live[:, None, None]

        table = lax.map(one_sink, jnp.arange(T_SIZE).astype(jnp.int32))
        return jnp.transpose(table, (1, 0, 2, 3))

    return lax.map(one_owner, jnp.arange(OPS).astype(jnp.int32))
```

```python
import functools

import jax
import jax.numpy as jnp
from jax import lax
from jax.experimental import pallas as pl
from jax.experimental.pallas import tpu as pltpu
from jax.sharding import PartitionSpec as P

MESH = pl.DeviceIdType.MESH
f32 = jnp.float32
bf16 = jnp.bfloat16


def flip(q, d, n):
    out = 0
    bit = 1
    while bit < n:
        digit = (q // bit) % 2
        out = out + bit * ((digit + (d // bit) % 2) % 2)
        bit *= 2
    return out


def halves(x):
    hi = x.astype(bf16)
    lo = (x - hi.astype(f32)).astype(bf16)
    return hi, lo


def put_wide(ref, k, x):
    n = x.shape[1]
    hi, lo = halves(x)
    ref[k, :, 0:n] = hi
    ref[k, :, n:2 * n] = lo


def put_tall(ref, k, x):
    n = x.shape[0]
    hi, lo = halves(x)
    ref[k, 0:n, :] = hi
    ref[k, n:2 * n, :] = lo


def mm(a_ref, b_ref, k):
    n = b_ref.shape[-1]
    left = jnp.concatenate([a_ref[k, :, 0:n], a_ref[k, :, n:2 * n], a_ref[k, :, 0:n]], axis=1)
    right = jnp.concatenate([b_ref[k, 0:n, :], b_ref[k, 0:n, :], b_ref[k, n:2 * n, :]], axis=0)
    return jnp.dot(left, right, preferred_element_type=f32)


def mm_t(a_ref, ka, b_ref, kb):
    n = b_ref.shape[1]
    left = jnp.concatenate([a_ref[ka, :, 0:n], a_ref[ka, :, n:2 * n], a_ref[ka, :, 0:n]], axis=1)
    right = jnp.concatenate([b_ref[kb, :, 0:n], b_ref[kb, :, 0:n], b_ref[kb, :, n:2 * n]], axis=1)
    return lax.dot_general(left, right, (((1,), (1,)), ((), ())), preferred_element_type=f32)


def kernel(ntm, nop, slots, order,
           pl_ref, pc_ref, p_hbm, s_hbm, k_hbm, out_ref,
           p_buf, s_buf, k_buf, x_buf, kk_buf, pp_buf, a_buf, b_buf, tr_buf,
           p_sem, own_sem, s_send, s_recv, f_send, d_send, d_recv, k_send, k_recv):
    nq = ntm // 2
    me = lax.axis_index("tm")
    z = lax.axis_index("op")
    q = me // 2
    c = me % 2
    sib = q * 2 + (1 - c)

    def chip(d):
        return flip(q, d, nq)

    def time_of(j):
        return chip(j // 2) * 2 + (c + j % 2) % 2

    def p_copy(t):
        return pltpu.make_async_copy(p_hbm.at[t], p_buf.at[t], p_sem.at[t])

    s_own = pltpu.make_async_copy(s_hbm, s_buf.at[0, 0], own_sem.at[0])
    k_own = pltpu.make_async_copy(k_hbm, k_buf.at[z], own_sem.at[1])
    k_own.start()
    s_own.start()
    for t in range(ntm):
        p_copy(t).start()

    barrier = pltpu.get_barrier_semaphore()
    pl.semaphore_signal(barrier, inc=1, device_id=(sib, z), device_id_type=MESH)
    for d in range(1, nq):
        pl.semaphore_signal(barrier, inc=1, device_id=(chip(d) * 2 + c, z), device_id_type=MESH)
    has = (z >= 1, z + 1 < nop)

    @pl.when(has[0])
    def _():
        pl.semaphore_signal(barrier, inc=1, device_id=(me, z - 1), device_id_type=MESH)

    @pl.when(has[1])
    def _():
        pl.semaphore_signal(barrier, inc=1, device_id=(me, z + 1), device_id_type=MESH)

    neighbours = jnp.where(z >= 1, 1, 0) + jnp.where(z + 1 < nop, 1, 0)
    pl.semaphore_wait(barrier, nq + neighbours)

    def k_copy(direction, h, chunk, src):
        b = z + (h - 1) * (1 - 2 * direction)
        to = z - 1 + 2 * direction
        return pltpu.make_async_remote_copy(
            src_ref=src if src is not None else k_buf.at[b, chunk],
            dst_ref=k_buf.at[b, chunk],
            send_sem=k_send.at[direction, h - 1, chunk],
            recv_sem=k_recv.at[direction, h - 1, chunk],
            device_id=(me, to), device_id_type=MESH)

    def k_arrival(direction, h, chunk):
        b = z + h * (1 - 2 * direction)
        return pltpu.make_async_remote_copy(
            src_ref=k_buf.at[b, chunk], dst_ref=k_buf.at[b, chunk],
            send_sem=k_send.at[direction, h - 1, chunk],
            recv_sem=k_recv.at[direction, h - 1, chunk],
            device_id=(me, z), device_id_type=MESH)

    def comes(direction, h):
        return z + h < nop if direction == 0 else z - h >= 0

    def sends(direction, h):
        return ((z + h - 1 < nop) & has[0]) if direction == 0 else ((z - h + 1 >= 0) & has[1])

    def own_k(direction, chunk):
        return k_copy(direction, 1, chunk, k_hbm.at[chunk])

    for chunk in range(2):
        for direction in range(2):
            @pl.when(sends(direction, 1))
            def _():
                own_k(direction, chunk).start()

    def s_copy(d):
        return pltpu.make_async_remote_copy(
            src_ref=s_hbm, dst_ref=s_buf.at[0, d],
            send_sem=s_send.at[d], recv_sem=s_recv.at[0, d],
            device_id=(chip(d) * 2 + c, z), device_id_type=MESH)

    def f_copy(d):
        return pltpu.make_async_remote_copy(
            src_ref=s_hbm if d == 0 else s_buf.at[0, d], dst_ref=s_buf.at[1, d],
            send_sem=f_send.at[d], recv_sem=s_recv.at[1, d],
            device_id=(sib, z), device_id_type=MESH)

    across = nq == 4
    near = list(range(1, 3 if across else nq))

    def d_copy(half):
        return pltpu.make_async_remote_copy(
            src_ref=s_buf.at[0, 2 - half, half], dst_ref=s_buf.at[0, 3, half],
            send_sem=d_send.at[half], recv_sem=d_recv.at[half],
            device_id=(chip(1 + half) * 2 + c, z), device_id_type=MESH)

    f_copy(0).start()
    for d in near:
        s_copy(d).start()

    def take_k(h, chunk):
        if h >= nop:
            return
        for direction in range(2):
            @pl.when(comes(direction, h))
            def _():
                k_arrival(direction, h, chunk).wait_recv()
            if h < nop - 1:
                @pl.when(comes(direction, h) & has[direction])
                def _():
                    k_copy(direction, h + 1, chunk, None).start()

    def split_k(b):
        re, im = k_buf[b, 0], k_buf[b, 1]
        put_tall(kk_buf.at[b], 0, re)
        put_tall(kk_buf.at[b], 1, im)
        put_tall(kk_buf.at[b], 2, re + im)

    def split_p(t):
        re, im = p_buf[t, 0], p_buf[t, 1]
        put_wide(pp_buf.at[t], 0, re)
        put_wide(pp_buf.at[t], 1, im)
        put_wide(pp_buf.at[t], 2, re + im)
        put_wide(pp_buf.at[t], 3, re - im)

    def make_x(j):
        pp = pp_buf.at[time_of(j)]
        s_re, s_im = s_buf[j % 2, j // 2, 0], s_buf[j % 2, j // 2, 1]
        put_tall(b_buf, 0, s_re)
        put_tall(b_buf, 1, s_im)
        put_tall(b_buf, 2, s_re + s_im)
        first = mm(pp, b_buf, 0)
        second = mm(pp, b_buf, 1)
        third = mm(pp, b_buf, 2)
        h_re = first - second
        h_im = third - first - second
        put_wide(a_buf, 0, h_re)
        put_wide(a_buf, 1, h_im)
        put_wide(a_buf, 2, h_re + h_im)
        first = mm_t(a_buf, 0, pp, 0)
        second = mm_t(a_buf, 1, pp, 1)
        third = mm_t(a_buf, 2, pp, 3)
        x_re = first + second
        x_im = third - first + second
        put_wide(x_buf.at[j], 0, x_re)
        put_wide(x_buf.at[j], 1, x_im)
        put_wide(x_buf.at[j], 2, x_re + x_im)

    def make_first(b, j):
        p_buf[j, 0] = mm(x_buf.at[j], kk_buf.at[b], 0)

    def make_z(b, j, ready=False):
        t = time_of(j)
        first = p_buf[j, 0] if ready else mm(x_buf.at[j], kk_buf.at[b], 0)
        second = mm(x_buf.at[j], kk_buf.at[b], 1)
        third = mm(x_buf.at[j], kk_buf.at[b], 2)
        z_re = first - second
        z_im = third - first - second
        re = jnp.sum((z_re + z_im) * (z_re - z_im).T, axis=0, keepdims=True)
        im = 2.0 * jnp.sum(z_re * z_im.T, axis=0, keepdims=True)
        row_re = re[:, 0:128]
        row_im = im[:, 0:128]
        for at in range(128, order, 128):
            row_re = row_re + re[:, at:at + 128]
            row_im = row_im + im[:, at:at + 128]
        tr_buf[b, 0, pl.ds(t, 1), :] = row_re
        tr_buf[b, 1, pl.ds(t, 1), :] = row_im

    def xs(lo, hi):
        lax.fori_loop(lo, hi, lambda j, _: (make_x(j), 0)[1], 0)

    def zs(reach_lo, reach_hi, lo, hi):
        pairs = (hi - lo) // 2
        reach_hi = min(reach_hi, nop - 1)
        if pairs == 0 or reach_lo > reach_hi:
            return

        def at(b, n):
            for k in range(2):
                make_z(b, lo + 2 * n + k)
            return 0

        if reach_lo == 0:
            b_lo = jnp.maximum(z - reach_hi, 0)
            b_hi = jnp.minimum(z + reach_hi, nop - 1) + 1
            lax.fori_loop(0, (b_hi - b_lo) * pairs, lambda n, _: at(b_lo + n // pairs, n % pairs), 0)
        else:
            def side(direction, _):
                b = z + reach_lo * (1 - 2 * direction)
                good = jnp.where((b >= 0) & (b < nop), 1, 0)
                lax.fori_loop(0, good * pairs, lambda n, _: at(b, n), 0)
                return 0

            lax.fori_loop(0, 2, side, 0)

    def split_new(h):
        if h >= nop:
            return

        def side(direction, _):
            b = z + h * (1 - 2 * direction)
            good = (b >= 0) & (b < nop)

            @pl.when(good)
            def _():
                split_k(b)

            return 0

        lax.fori_loop(0, 2, side, 0)

    k_own.wait()
    split_k(z)
    s_own.wait()
    for t in range(ntm):
        p_copy(t).wait()
    lax.fori_loop(0, 2, lambda j, _: (split_p(time_of(j)), 0)[1], 0)
    f_copy(0).wait_recv()
    xs(0, 2)
    zs(0, 0, 0, 2)
    lax.fori_loop(2, ntm, lambda j, _: (split_p(time_of(j)), 0)[1], 0)
    take_k(1, 0)
    for d in near:
        s_copy(d).wait_recv()
        f_copy(d).start()
        if across:
            d_copy(2 - d).start()
    take_k(1, 1)
    split_new(1)
    zs(1, 1, 0, 2)
    for d in near:
        f_copy(d).wait_recv()
    upto = 2 + 2 * len(near)
    xs(2, upto)
    zs(0, 0, 2, upto)
    take_k(2, 0)
    if across:
        for half in range(2):
            d_copy(half).wait_recv()
        f_copy(3).start()
    zs(1, 1, 2, upto)
    take_k(2, 1)
    split_new(2)
    zs(2, 2, 0, upto)
    if across:
        f_copy(3).wait_recv()
        xs(upto, ntm)
        zs(0, 2, upto, ntm)
    def last_side(h, step):
        def side(direction, _):
            b = z + h * (1 - 2 * direction)

            @pl.when((b >= 0) & (b < nop))
            def _():
                step(b)

            return 0

        lax.fori_loop(0, 2, side, 0)

    def by(group, b, work):
        def at(n, _):
            for k in range(group):
                work(b, group * n + k)
            return 0

        lax.fori_loop(0, ntm // group, at, 0)

    for h in range(3, nop):
        if h < nop - 1:
            take_k(h, 0)
            take_k(h, 1)
            split_new(h)
            zs(h, h, 0, ntm)
            continue

        def real_part(b):
            put_tall(kk_buf.at[b], 0, k_buf[b, 0])
            by(2, b, make_first)

        def the_rest(b):
            im = k_buf[b, 1]
            put_tall(kk_buf.at[b], 1, im)
            put_tall(kk_buf.at[b], 2, k_buf[b, 0] + im)
            by(4 if ntm % 4 == 0 else 2, b, lambda b, j: make_z(b, j, True))

        take_k(h, 0)
        last_side(h, real_part)
        take_k(h, 1)
        last_side(h, the_rest)

    table = [tr_buf[b] for b in range(nop)]
    rows = []
    for s in range(slots):
        picked = jnp.zeros_like(table[0])
        for b in range(nop):
            picked = jnp.where(pl_ref[s] == b, table[b], picked)
        picked = jnp.where(s < pc_ref[0], picked, 0.0)
        rows.append(picked.reshape(2 * ntm, 128))
    sums = lax.dot_general(
        jnp.ones((8, 128), f32), jnp.concatenate(rows, axis=0), (((1,), (1,)), ((), ())),
        precision=lax.Precision.HIGHEST, preferred_element_type=f32)
    for r in range(2 * slots):
        out_ref[r:r + 1, :] = sums[0:1, r * ntm:r * ntm + ntm]

    for d in near:
        s_copy(d).wait_send()
    if across:
        for half in range(2):
            d_copy(half).wait_send()
    for d in range(nq):
        f_copy(d).wait_send()
    for direction in range(2):
        for h in range(1, nop):
            @pl.when(sends(direction, h))
            def _():
                for chunk in range(2):
                    k_copy(direction, h, chunk, k_hbm.at[chunk] if h == 1 else None).wait_send()


def body(ntm, nop, perambs, src_ops, sink_ops, pair_list, pair_count):
    order = perambs.shape[-1]
    slots = pair_list.shape[1]
    times = perambs.shape[1]
    nq = ntm // 2
    block = (2, order, order)
    parts = pl.pallas_call(
        functools.partial(kernel, ntm, nop, slots, order),
        out_shape=pltpu.VMEM((2 * slots, times), f32),
        in_specs=[pl.BlockSpec(memory_space=pltpu.SMEM)] * 2 + [pl.BlockSpec(memory_space=pl.ANY)] * 3,
        out_specs=pl.BlockSpec(memory_space=pltpu.VMEM),
        scratch_shapes=[
            pltpu.VMEM((times,) + block, f32),
            pltpu.VMEM((2, nq) + block, f32),
            pltpu.VMEM((nop,) + block, f32),
            pltpu.VMEM((times, 3, order, 2 * order), bf16),
            pltpu.VMEM((nop, 3, 2 * order, order), bf16),
            pltpu.VMEM((times, 4, order, 2 * order), bf16),
            pltpu.VMEM((3, order, 2 * order), bf16),
            pltpu.VMEM((3, 2 * order, order), bf16),
            pltpu.VMEM((nop, 2, times, 128), f32),
            pltpu.SemaphoreType.DMA((times,)),
            pltpu.SemaphoreType.DMA((2,)),
            pltpu.SemaphoreType.DMA((nq,)),
            pltpu.SemaphoreType.DMA((2, nq)),
            pltpu.SemaphoreType.DMA((nq,)),
            pltpu.SemaphoreType.DMA((2,)),
            pltpu.SemaphoreType.DMA((2,)),
            pltpu.SemaphoreType.DMA((2, nop, 2)),
            pltpu.SemaphoreType.DMA((2, nop, 2)),
        ],
        compiler_params=pltpu.CompilerParams(
            collective_id=0, has_side_effects=True, vmem_limit_bytes=64 * 1000 * 1000),
    )(pair_list[0], pair_count, perambs[0], src_ops[0, 0], sink_ops[0, 0])
    return parts.reshape(1, slots, 1, 2, times)


def solution(mesh):
    placed = (
        P("tm", None, None, None, None),
        P("op", "tm", None, None, None),
        P("op", "tm", None, None, None),
        P("op", None),
        P("op"),
    )
    return jax.shard_map(
        functools.partial(body, mesh.shape["tm"], mesh.shape["op"]),
        mesh=mesh, in_specs=placed, out_specs=P("op", None, "tm", None, None), check_vma=False
    )
```

```python
import functools

import jax
import jax.numpy as jnp
from jax import lax
from jax.experimental import pallas as pl
from jax.experimental.pallas import tpu as pltpu
from jax.sharding import PartitionSpec as P

MESH = pl.DeviceIdType.MESH
f32 = jnp.float32
bf16 = jnp.bfloat16


def flip(q, d, n):
    out = 0
    bit = 1
    while bit < n:
        digit = (q // bit) % 2
        out = out + bit * ((digit + (d // bit) % 2) % 2)
        bit *= 2
    return out


def halves(x):
    hi = x.astype(bf16)
    lo = (x - hi.astype(f32)).astype(bf16)
    return hi, lo


def put_wide(ref, k, x):
    n = x.shape[1]
    hi, lo = halves(x)
    ref[k, :, 0:n] = hi
    ref[k, :, n:2 * n] = lo


def put_tall(ref, k, x):
    n = x.shape[0]
    hi, lo = halves(x)
    ref[k, 0:n, :] = hi
    ref[k, n:2 * n, :] = lo


def mm(a_ref, b_ref, k):
    n = b_ref.shape[-1]
    left = jnp.concatenate([a_ref[k, :, 0:n], a_ref[k, :, n:2 * n], a_ref[k, :, 0:n]], axis=1)
    right = jnp.concatenate([b_ref[k, 0:n, :], b_ref[k, 0:n, :], b_ref[k, n:2 * n, :]], axis=0)
    return jnp.dot(left, right, preferred_element_type=f32)


def mm_t(a_ref, ka, b_ref, kb):
    n = b_ref.shape[1]
    left = jnp.concatenate([a_ref[ka, :, 0:n], a_ref[ka, :, n:2 * n], a_ref[ka, :, 0:n]], axis=1)
    right = jnp.concatenate([b_ref[kb, :, 0:n], b_ref[kb, :, 0:n], b_ref[kb, :, n:2 * n]], axis=1)
    return lax.dot_general(left, right, (((1,), (1,)), ((), ())), preferred_element_type=f32)


def kernel(ntm, nop, slots, order,
           pl_ref, pc_ref, p_hbm, s_hbm, k_hbm, out_ref,
           p_buf, s_buf, k_buf, x_buf, kk_buf, pp_buf, a_buf, b_buf, tr_buf,
           p_sem, own_sem, s_send, s_recv, f_send, d_send, d_recv, k_send, k_recv):
    nq = ntm // 2
    me = lax.axis_index("tm")
    z = lax.axis_index("op")
    q = me // 2
    c = me % 2
    sib = q * 2 + (1 - c)

    def chip(d):
        return flip(q, d, nq)

    def time_of(j):
        return chip(j // 2) * 2 + (c + j % 2) % 2

    def p_copy(t):
        return pltpu.make_async_copy(p_hbm.at[t], p_buf.at[t], p_sem.at[t])

    barrier = pltpu.get_barrier_semaphore()
    pl.semaphore_signal(barrier, inc=1, device_id=(sib, z), device_id_type=MESH)
    across = nq == 4
    near = list(range(1, 3 if across else nq))
    for d in near:
        pl.semaphore_signal(barrier, inc=1, device_id=(chip(d) * 2 + c, z), device_id_type=MESH)
    has = (z >= 1, z + 1 < nop)

    @pl.when(has[0])
    def _():
        pl.semaphore_signal(barrier, inc=1, device_id=(me, z - 1), device_id_type=MESH)

    @pl.when(has[1])
    def _():
        pl.semaphore_signal(barrier, inc=1, device_id=(me, z + 1), device_id_type=MESH)

    s_own = pltpu.make_async_copy(s_hbm, s_buf.at[0, 0], own_sem.at[0])
    k_own = pltpu.make_async_copy(k_hbm, k_buf.at[z], own_sem.at[1])
    k_own.start()
    s_own.start()
    for t in range(ntm):
        p_copy(t).start()

    neighbours = jnp.where(z >= 1, 1, 0) + jnp.where(z + 1 < nop, 1, 0)
    pl.semaphore_wait(barrier, 1 + len(near) + neighbours)

    strip = order // 2
    pieces = [(0, 0, strip), (0, strip, strip), (1, 0, strip), (1, strip, strip)]

    def piece(ref, n):
        part, lo, size = pieces[n]
        return ref.at[part, pl.ds(lo, size)]

    def k_copy(direction, h, chunk, own=False):
        b = z + (h - 1) * (1 - 2 * direction)
        to = z - 1 + 2 * direction
        return pltpu.make_async_remote_copy(
            src_ref=piece(k_hbm if own else k_buf.at[b], chunk),
            dst_ref=piece(k_buf.at[b], chunk),
            send_sem=k_send.at[direction, h - 1, chunk],
            recv_sem=k_recv.at[direction, h - 1, chunk],
            device_id=(me, to), device_id_type=MESH)

    def k_arrival(direction, h, chunk):
        b = z + h * (1 - 2 * direction)
        return pltpu.make_async_remote_copy(
            src_ref=piece(k_buf.at[b], chunk), dst_ref=piece(k_buf.at[b], chunk),
            send_sem=k_send.at[direction, h - 1, chunk],
            recv_sem=k_recv.at[direction, h - 1, chunk],
            device_id=(me, z), device_id_type=MESH)

    def comes(direction, h):
        return z + h < nop if direction == 0 else z - h >= 0

    def sends(direction, h):
        return ((z + h - 1 < nop) & has[0]) if direction == 0 else ((z - h + 1 >= 0) & has[1])

    def own_k(direction, chunk):
        return k_copy(direction, 1, chunk, True)

    for chunk in range(len(pieces)):
        for direction in range(2):
            @pl.when(sends(direction, 1))
            def _():
                own_k(direction, chunk).start()

    def s_copy(d):
        return pltpu.make_async_remote_copy(
            src_ref=s_hbm, dst_ref=s_buf.at[0, d],
            send_sem=s_send.at[d], recv_sem=s_recv.at[0, d],
            device_id=(chip(d) * 2 + c, z), device_id_type=MESH)

    def f_copy(d):
        return pltpu.make_async_remote_copy(
            src_ref=s_hbm if d == 0 else s_buf.at[0, d], dst_ref=s_buf.at[1, d],
            send_sem=f_send.at[d], recv_sem=s_recv.at[1, d],
            device_id=(sib, z), device_id_type=MESH)

    def d_copy(half):
        return pltpu.make_async_remote_copy(
            src_ref=s_buf.at[0, 2 - half, half], dst_ref=s_buf.at[0, 3, half],
            send_sem=d_send.at[half], recv_sem=d_recv.at[half],
            device_id=(chip(1 + half) * 2 + c, z), device_id_type=MESH)

    f_copy(0).start()
    for d in near:
        s_copy(d).start()

    def take_k(h, chunk):
        if h >= nop:
            return
        for direction in range(2):
            @pl.when(comes(direction, h))
            def _():
                k_arrival(direction, h, chunk).wait_recv()
            if h < nop - 1:
                @pl.when(comes(direction, h) & has[direction])
                def _():
                    k_copy(direction, h + 1, chunk).start()

    def split_k(b):
        re, im = k_buf[b, 0], k_buf[b, 1]
        put_tall(kk_buf.at[b], 0, re)
        put_tall(kk_buf.at[b], 1, im)
        put_tall(kk_buf.at[b], 2, re + im)

    def split_p(t):
        re, im = p_buf[t, 0], p_buf[t, 1]
        put_wide(pp_buf.at[t], 0, re)
        put_wide(pp_buf.at[t], 1, im)
        put_wide(pp_buf.at[t], 2, re + im)
        put_wide(pp_buf.at[t], 3, re - im)

    def make_x(j):
        pp = pp_buf.at[time_of(j)]
        s_re, s_im = s_buf[j % 2, j // 2, 0], s_buf[j % 2, j // 2, 1]
        put_tall(b_buf, 0, s_re)
        put_tall(b_buf, 1, s_im)
        put_tall(b_buf, 2, s_re + s_im)
        first = mm(pp, b_buf, 0)
        second = mm(pp, b_buf, 1)
        third = mm(pp, b_buf, 2)
        h_re = first - second
        h_im = third - first - second
        put_wide(a_buf, 0, h_re)
        put_wide(a_buf, 1, h_im)
        put_wide(a_buf, 2, h_re + h_im)
        first = mm_t(a_buf, 0, pp, 0)
        second = mm_t(a_buf, 1, pp, 1)
        third = mm_t(a_buf, 2, pp, 3)
        x_re = first + second
        x_im = third - first + second
        put_wide(x_buf.at[j], 0, x_re)
        put_wide(x_buf.at[j], 1, x_im)
        put_wide(x_buf.at[j], 2, x_re + x_im)

    def make_z(b, j):
        first = mm(x_buf.at[j], kk_buf.at[b], 0)
        second = mm(x_buf.at[j], kk_buf.at[b], 1)
        third = mm(x_buf.at[j], kk_buf.at[b], 2)
        z_re = first - second
        z_im = third - first - second
        trace(b, j, z_re, z_im)

    def trace(b, j, z_re, z_im):
        t = time_of(j)
        cut = [slice(at, at + 128) for at in range(0, order, 128)]
        re = im = None
        for n, top in enumerate(cut):
            for side in cut[n:]:
                a, b_ = z_re[top, side], z_im[top, side]
                at, bt = z_re[side, top].T, z_im[side, top].T
                now_re = a * at - b_ * bt
                now_im = a * bt + b_ * at if side != top else a * bt
                now_re = now_re if side == top else 2.0 * now_re
                re = now_re if re is None else re + now_re
                im = now_im if im is None else im + now_im
        row_re = jnp.sum(re, axis=0, keepdims=True)
        row_im = 2.0 * jnp.sum(im, axis=0, keepdims=True)
        tr_buf[b, 0, pl.ds(t, 1), :] = row_re
        tr_buf[b, 1, pl.ds(t, 1), :] = row_im

    def xs(lo, hi):
        lax.fori_loop(lo, hi, lambda j, _: (make_x(j), 0)[1], 0)

    def zs(reach_lo, reach_hi, lo, hi):
        pairs = (hi - lo) // 2
        reach_hi = min(reach_hi, nop - 1)
        if pairs == 0 or reach_lo > reach_hi:
            return

        def at(b, n):
            for k in range(2):
                make_z(b, lo + 2 * n + k)
            return 0

        if reach_lo == 0:
            b_lo = jnp.maximum(z - reach_hi, 0)
            b_hi = jnp.minimum(z + reach_hi, nop - 1) + 1
            lax.fori_loop(0, (b_hi - b_lo) * pairs, lambda n, _: at(b_lo + n // pairs, n % pairs), 0)
        else:
            def side(direction, _):
                b = z + reach_lo * (1 - 2 * direction)
                good = jnp.where((b >= 0) & (b < nop), 1, 0)
                lax.fori_loop(0, good * pairs, lambda n, _: at(b, n), 0)
                return 0

            lax.fori_loop(0, 2, side, 0)

    def split_new(h):
        if h >= nop:
            return

        def side(direction, _):
            b = z + h * (1 - 2 * direction)
            good = (b >= 0) & (b < nop)

            @pl.when(good)
            def _():
                split_k(b)

            return 0

        lax.fori_loop(0, 2, side, 0)

    k_own.wait()
    split_k(z)
    s_own.wait()
    for t in range(ntm):
        p_copy(t).wait()
    lax.fori_loop(0, 2, lambda j, _: (split_p(time_of(j)), 0)[1], 0)
    f_copy(0).wait_recv()
    xs(0, 2)
    zs(0, 0, 0, 2)
    lax.fori_loop(2, ntm, lambda j, _: (split_p(time_of(j)), 0)[1], 0)
    take_k(1, 0)
    take_k(1, 1)
    for d in near:
        s_copy(d).wait_recv()
        f_copy(d).start()
        if across:
            d_copy(2 - d).start()
    take_k(1, 2)
    take_k(1, 3)
    split_new(1)
    zs(1, 1, 0, 2)
    for d in near:
        f_copy(d).wait_recv()
    upto = 2 + 2 * len(near)
    xs(2, upto)
    zs(0, 0, 2, upto)
    take_k(2, 0)
    take_k(2, 1)
    if across:
        for half in range(2):
            d_copy(half).wait_recv()
        f_copy(3).start()
    zs(1, 1, 2, upto)
    take_k(2, 2)
    take_k(2, 3)
    split_new(2)
    zs(2, 2, 0, upto)
    if across:
        f_copy(3).wait_recv()
        xs(upto, ntm)
        zs(0, 2, upto, ntm)
    def last_side(h, step):
        def side(direction, _):
            b = z + h * (1 - 2 * direction)

            @pl.when((b >= 0) & (b < nop))
            def _():
                step(b)

            return 0

        lax.fori_loop(0, 2, side, 0)

    def by(group, b, work):
        def at(n, _):
            for k in range(group):
                work(b, group * n + k)
            return 0

        lax.fori_loop(0, ntm // group, at, 0)

    for h in range(3, nop):
        if h < nop - 1:
            for chunk in range(len(pieces)):
                take_k(h, chunk)
            split_new(h)
            zs(h, h, 0, ntm)
            continue

        def put_piece(b, n):
            k, lo, size = pieces[n]
            hi, small = halves(k_buf[b, k, lo:lo + size, :])
            kk_buf[b, k, lo:lo + size, :] = hi
            kk_buf[b, k, order + lo:order + lo + size, :] = small

        def right_of(b, k, lo, size):
            hi, small = kk_buf[b, k, lo:lo + size, :], kk_buf[b, k, order + lo:order + lo + size, :]
            return jnp.concatenate([hi, hi, small], axis=0)

        def left_of(j, x, lo, size):
            hi, small = x_buf[j, x, :, lo:lo + size], x_buf[j, x, :, order + lo:order + lo + size]
            return jnp.concatenate([hi, small, hi], axis=1)

        def dot(left, right):
            return jnp.dot(left, right, preferred_element_type=f32)

        def real_part(b):
            put_piece(b, 0)
            put_piece(b, 1)
            right = right_of(b, 0, 0, order)

            def step(b, j):
                p_buf[j, 0] = dot(left_of(j, 0, 0, order), right)
                p_buf[j, 1] = dot(left_of(j, 1, 0, order), right)

            by(ntm, b, step)

        def upper_part(b):
            put_piece(b, 2)
            right = right_of(b, 1, 0, strip)

            def step(b, j):
                p_buf[j, 0] = p_buf[j, 0] - dot(left_of(j, 1, 0, strip), right)
                p_buf[j, 1] = p_buf[j, 1] + dot(left_of(j, 0, 0, strip), right)

            by(ntm, b, step)

        def last_part(b):
            put_piece(b, 3)
            right = right_of(b, 1, strip, strip)

            def step(b, j):
                z_re = p_buf[j, 0] - dot(left_of(j, 1, strip, strip), right)
                z_im = p_buf[j, 1] + dot(left_of(j, 0, strip, strip), right)
                trace(b, j, z_re, z_im)

            by(ntm, b, step)

        take_k(h, 0)
        take_k(h, 1)
        last_side(h, real_part)
        take_k(h, 2)
        last_side(h, upper_part)
        take_k(h, 3)
        last_side(h, last_part)

    at_row = lax.broadcasted_iota(jnp.int32, (ntm, ntm), 0)
    at_lane = lax.broadcasted_iota(jnp.int32, (ntm, ntm), 1)

    def total(b, part):
        sums = jnp.sum(tr_buf[b, part], axis=1, keepdims=True)
        return jnp.sum(jnp.where(at_row == at_lane, sums, 0.0), axis=0, keepdims=True)

    table = [[total(b, part) for part in range(2)] for b in range(nop)]
    for s in range(slots):
        for part in range(2):
            picked = jnp.zeros((1, ntm), f32)
            for b in range(nop):
                picked = jnp.where(pl_ref[s] == b, table[b][part], picked)
            out_ref[2 * s + part:2 * s + part + 1, :] = jnp.where(s < pc_ref[0], picked, 0.0)

    for d in near:
        s_copy(d).wait_send()
    if across:
        for half in range(2):
            d_copy(half).wait_send()
    for d in range(nq):
        f_copy(d).wait_send()
    for direction in range(2):
        for h in range(1, nop):
            @pl.when(sends(direction, h))
            def _():
                for chunk in range(len(pieces)):
                    k_copy(direction, h, chunk, h == 1).wait_send()


def body(ntm, nop, perambs, src_ops, sink_ops, pair_list, pair_count):
    order = perambs.shape[-1]
    slots = pair_list.shape[1]
    times = perambs.shape[1]
    nq = ntm // 2
    block = (2, order, order)
    parts = pl.pallas_call(
        functools.partial(kernel, ntm, nop, slots, order),
        out_shape=pltpu.VMEM((2 * slots, times), f32),
        in_specs=[pl.BlockSpec(memory_space=pltpu.SMEM)] * 2 + [pl.BlockSpec(memory_space=pl.ANY)] * 3,
        out_specs=pl.BlockSpec(memory_space=pltpu.VMEM),
        scratch_shapes=[
            pltpu.VMEM((times,) + block, f32),
            pltpu.VMEM((2, nq) + block, f32),
            pltpu.VMEM((nop,) + block, f32),
            pltpu.VMEM((times, 3, order, 2 * order), bf16),
            pltpu.VMEM((nop, 3, 2 * order, order), bf16),
            pltpu.VMEM((times, 4, order, 2 * order), bf16),
            pltpu.VMEM((3, order, 2 * order), bf16),
            pltpu.VMEM((3, 2 * order, order), bf16),
            pltpu.VMEM((nop, 2, times, 128), f32),
            pltpu.SemaphoreType.DMA((times,)),
            pltpu.SemaphoreType.DMA((2,)),
            pltpu.SemaphoreType.DMA((nq,)),
            pltpu.SemaphoreType.DMA((2, nq)),
            pltpu.SemaphoreType.DMA((nq,)),
            pltpu.SemaphoreType.DMA((2,)),
            pltpu.SemaphoreType.DMA((2,)),
            pltpu.SemaphoreType.DMA((2, nop, 4)),
            pltpu.SemaphoreType.DMA((2, nop, 4)),
        ],
        compiler_params=pltpu.CompilerParams(
            collective_id=0, has_side_effects=True, vmem_limit_bytes=64 * 1000 * 1000),
    )(pair_list[0], pair_count, perambs[0], src_ops[0, 0], sink_ops[0, 0])
    return parts.reshape(1, slots, 1, 2, times)


def solution(mesh):
    placed = (
        P("tm", None, None, None, None),
        P("op", "tm", None, None, None),
        P("op", "tm", None, None, None),
        P("op", None),
        P("op"),
    )
    return jax.shard_map(
        functools.partial(body, mesh.shape["tm"], mesh.shape["op"]),
        mesh=mesh, in_specs=placed, out_specs=P("op", None, "tm", None, None), check_vma=False
    )
```

```python
import functools

import jax
import jax.numpy as jnp
from jax import lax
from jax.experimental import pallas as pl
from jax.experimental.pallas import tpu as pltpu
from jax.sharding import PartitionSpec as P

MESH = pl.DeviceIdType.MESH
f32 = jnp.float32
bf16 = jnp.bfloat16


def flip(q, d, n):
    out = 0
    bit = 1
    while bit < n:
        digit = (q // bit) % 2
        out = out + bit * ((digit + (d // bit) % 2) % 2)
        bit *= 2
    return out


def halves(x):
    hi = x.astype(bf16)
    lo = (x - hi.astype(f32)).astype(bf16)
    return hi, lo


def put_wide(ref, k, x):
    n = x.shape[1]
    hi, lo = halves(x)
    ref[k, :, 0:n] = hi
    ref[k, :, n:2 * n] = lo


def put_tall(ref, k, x):
    n = x.shape[0]
    hi, lo = halves(x)
    ref[k, 0:n, :] = hi
    ref[k, n:2 * n, :] = lo


def mm(a_ref, b_ref, k):
    n = b_ref.shape[-1]
    left = jnp.concatenate([a_ref[k, :, 0:n], a_ref[k, :, n:2 * n], a_ref[k, :, 0:n]], axis=1)
    right = jnp.concatenate([b_ref[k, 0:n, :], b_ref[k, 0:n, :], b_ref[k, n:2 * n, :]], axis=0)
    return jnp.dot(left, right, preferred_element_type=f32)


def mm_t(a_ref, ka, b_ref, kb):
    n = b_ref.shape[1]
    left = jnp.concatenate([a_ref[ka, :, 0:n], a_ref[ka, :, n:2 * n], a_ref[ka, :, 0:n]], axis=1)
    right = jnp.concatenate([b_ref[kb, :, 0:n], b_ref[kb, :, 0:n], b_ref[kb, :, n:2 * n]], axis=1)
    return lax.dot_general(left, right, (((1,), (1,)), ((), ())), preferred_element_type=f32)


def kernel(ntm, nop, slots, order,
           pl_hbm, pc_hbm, p_hbm, s_hbm, k_hbm, out_ref,
           p_buf, s_buf, k_buf, x_buf, kk_buf, pp_buf, a_buf, b_buf, tr_buf, pl_ref, pc_ref,
           list_sem, p_sem, own_sem, s_send, s_recv, f_send, d_send, d_recv, k_send, k_recv):
    nq = ntm // 2
    me = lax.axis_index("tm")
    z = lax.axis_index("op")
    q = me // 2
    c = me % 2
    sib = q * 2 + (1 - c)

    def chip(d):
        return flip(q, d, nq)

    def time_of(j):
        return chip(j // 2) * 2 + (c + j % 2) % 2

    def p_copy(t):
        return pltpu.make_async_copy(p_hbm.at[t], p_buf.at[t], p_sem.at[t])

    barrier = pltpu.get_barrier_semaphore()
    pl.semaphore_signal(barrier, inc=1, device_id=(sib, z), device_id_type=MESH)
    across = nq == 4
    near = list(range(1, 3 if across else nq))
    for d in near:
        pl.semaphore_signal(barrier, inc=1, device_id=(chip(d) * 2 + c, z), device_id_type=MESH)
    has = (z >= 1, z + 1 < nop)

    @pl.when(has[0])
    def _():
        pl.semaphore_signal(barrier, inc=1, device_id=(me, z - 1), device_id_type=MESH)

    @pl.when(has[1])
    def _():
        pl.semaphore_signal(barrier, inc=1, device_id=(me, z + 1), device_id_type=MESH)

    s_own = pltpu.make_async_copy(s_hbm, s_buf.at[0, 0], own_sem.at[0])
    k_own = pltpu.make_async_copy(k_hbm, k_buf.at[z], own_sem.at[1])
    k_own.start()
    s_own.start()
    lists = [pltpu.make_async_copy(pl_hbm, pl_ref, list_sem.at[0]), pltpu.make_async_copy(pc_hbm, pc_ref, list_sem.at[1])]
    for copy in lists:
        copy.start()
    for t in range(ntm):
        p_copy(t).start()

    neighbours = jnp.where(z >= 1, 1, 0) + jnp.where(z + 1 < nop, 1, 0)
    pl.semaphore_wait(barrier, 1 + len(near) + neighbours)

    strip = order // 2
    coarse = [(0, 0, order), (1, 0, order)]
    fine = [(0, 0, order), (1, 0, strip), (1, strip, strip)]

    def pieces(h):
        return fine if h == nop - 1 and h >= 3 else coarse

    def piece(ref, h, n):
        part, lo, size = pieces(h)[n]
        return ref.at[part, pl.ds(lo, size)]

    def k_copy(direction, h, chunk, own=False):
        b = z + (h - 1) * (1 - 2 * direction)
        to = z - 1 + 2 * direction
        return pltpu.make_async_remote_copy(
            src_ref=piece(k_hbm if own else k_buf.at[b], h, chunk),
            dst_ref=piece(k_buf.at[b], h, chunk),
            send_sem=k_send.at[direction, h - 1, chunk],
            recv_sem=k_recv.at[direction, h - 1, chunk],
            device_id=(me, to), device_id_type=MESH)

    def k_arrival(direction, h, chunk):
        b = z + h * (1 - 2 * direction)
        return pltpu.make_async_remote_copy(
            src_ref=piece(k_buf.at[b], h, chunk), dst_ref=piece(k_buf.at[b], h, chunk),
            send_sem=k_send.at[direction, h - 1, chunk],
            recv_sem=k_recv.at[direction, h - 1, chunk],
            device_id=(me, z), device_id_type=MESH)

    def comes(direction, h):
        return z + h < nop if direction == 0 else z - h >= 0

    def sends(direction, h):
        return ((z + h - 1 < nop) & has[0]) if direction == 0 else ((z - h + 1 >= 0) & has[1])

    def own_k(direction, chunk):
        return k_copy(direction, 1, chunk, True)

    def s_copy(d):
        return pltpu.make_async_remote_copy(
            src_ref=s_hbm, dst_ref=s_buf.at[0, d],
            send_sem=s_send.at[d], recv_sem=s_recv.at[0, d],
            device_id=(chip(d) * 2 + c, z), device_id_type=MESH)

    def f_copy(d):
        return pltpu.make_async_remote_copy(
            src_ref=s_hbm if d == 0 else s_buf.at[0, d], dst_ref=s_buf.at[1, d],
            send_sem=f_send.at[d], recv_sem=s_recv.at[1, d],
            device_id=(sib, z), device_id_type=MESH)

    def d_copy(half):
        return pltpu.make_async_remote_copy(
            src_ref=s_buf.at[0, 2 - half, half], dst_ref=s_buf.at[0, 3, half],
            send_sem=d_send.at[half], recv_sem=d_recv.at[half],
            device_id=(chip(1 + half) * 2 + c, z), device_id_type=MESH)

    for chunk in range(len(pieces(1))):
        for direction in range(2):
            @pl.when(sends(direction, 1) & (c == 0))
            def _():
                own_k(direction, chunk).start()

    f_copy(0).start()
    for d in near:
        s_copy(d).start()
    for chunk in range(len(pieces(1))):
        for direction in range(2):
            @pl.when(sends(direction, 1) & (c == 1))
            def _():
                own_k(direction, chunk).start()


    def take_k(h, chunk):
        if h >= nop:
            return
        for direction in range(2):
            @pl.when(comes(direction, h))
            def _():
                k_arrival(direction, h, chunk).wait_recv()
            if h < nop - 1:
                @pl.when(comes(direction, h) & has[direction])
                def _():
                    for n, (part, _, _) in enumerate(pieces(h + 1)):
                        if part == pieces(h)[chunk][0]:
                            k_copy(direction, h + 1, n).start()

    def split_k(b):
        re, im = k_buf[b, 0], k_buf[b, 1]
        put_tall(kk_buf.at[b], 0, re)
        put_tall(kk_buf.at[b], 1, im)
        put_tall(kk_buf.at[b], 2, re + im)

    def split_p(t):
        re, im = p_buf[t, 0], p_buf[t, 1]
        put_wide(pp_buf.at[t], 0, re)
        put_wide(pp_buf.at[t], 1, im)
        put_wide(pp_buf.at[t], 2, re + im)
        put_wide(pp_buf.at[t], 3, re - im)

    def make_x(j):
        pp = pp_buf.at[time_of(j)]
        s_re, s_im = s_buf[j % 2, j // 2, 0], s_buf[j % 2, j // 2, 1]
        put_tall(b_buf, 0, s_re)
        put_tall(b_buf, 1, s_im)
        put_tall(b_buf, 2, s_re + s_im)
        first = mm(pp, b_buf, 0)
        second = mm(pp, b_buf, 1)
        third = mm(pp, b_buf, 2)
        h_re = first - second
        h_im = third - first - second
        put_wide(a_buf, 0, h_re)
        put_wide(a_buf, 1, h_im)
        put_wide(a_buf, 2, h_re + h_im)
        first = mm_t(a_buf, 0, pp, 0)
        second = mm_t(a_buf, 1, pp, 1)
        third = mm_t(a_buf, 2, pp, 3)
        x_re = first + second
        x_im = third - first + second
        put_wide(x_buf.at[j], 0, x_re)
        put_wide(x_buf.at[j], 1, x_im)
        put_wide(x_buf.at[j], 2, x_re + x_im)

    def make_z(b, j):
        first = mm(x_buf.at[j], kk_buf.at[b], 0)
        second = mm(x_buf.at[j], kk_buf.at[b], 1)
        third = mm(x_buf.at[j], kk_buf.at[b], 2)
        z_re = first - second
        z_im = third - first - second
        trace(b, j, z_re, z_im)

    def trace(b, j, z_re, z_im):
        t = time_of(j)
        cut = [slice(at, at + 128) for at in range(0, order, 128)]
        re = im = None
        for n, top in enumerate(cut):
            for side in cut[n:]:
                a, b_ = z_re[top, side], z_im[top, side]
                at, bt = z_re[side, top].T, z_im[side, top].T
                now_re = a * at - b_ * bt
                now_im = a * bt + b_ * at if side != top else a * bt
                now_re = now_re if side == top else 2.0 * now_re
                re = now_re if re is None else re + now_re
                im = now_im if im is None else im + now_im
        row_re = jnp.sum(re, axis=0, keepdims=True)
        row_im = 2.0 * jnp.sum(im, axis=0, keepdims=True)
        tr_buf[b, 0, pl.ds(t, 1), :] = row_re
        tr_buf[b, 1, pl.ds(t, 1), :] = row_im

    def xs(lo, hi):
        lax.fori_loop(lo, hi, lambda j, _: (make_x(j), 0)[1], 0)

    def zs(reach_lo, reach_hi, lo, hi):
        pairs = (hi - lo) // 2
        reach_hi = min(reach_hi, nop - 1)
        if pairs == 0 or reach_lo > reach_hi:
            return

        def at(b, n):
            for k in range(2):
                make_z(b, lo + 2 * n + k)
            return 0

        if reach_lo == 0:
            b_lo = jnp.maximum(z - reach_hi, 0)
            b_hi = jnp.minimum(z + reach_hi, nop - 1) + 1
            lax.fori_loop(0, (b_hi - b_lo) * pairs, lambda n, _: at(b_lo + n // pairs, n % pairs), 0)
        else:
            def side(direction, _):
                b = z + reach_lo * (1 - 2 * direction)
                good = jnp.where((b >= 0) & (b < nop), 1, 0)
                lax.fori_loop(0, good * pairs, lambda n, _: at(b, n), 0)
                return 0

            lax.fori_loop(0, 2, side, 0)

    def split_new(h):
        if h >= nop:
            return

        def side(direction, _):
            b = z + h * (1 - 2 * direction)
            good = (b >= 0) & (b < nop)

            @pl.when(good)
            def _():
                split_k(b)

            return 0

        lax.fori_loop(0, 2, side, 0)

    k_own.wait()
    split_k(z)
    s_own.wait()
    for t in range(ntm):
        p_copy(t).wait()
    lax.fori_loop(0, 2, lambda j, _: (split_p(time_of(j)), 0)[1], 0)
    f_copy(0).wait_recv()
    xs(0, 2)
    zs(0, 0, 0, 2)
    lax.fori_loop(2, ntm, lambda j, _: (split_p(time_of(j)), 0)[1], 0)
    take_k(1, 0)
    for d in near:
        s_copy(d).wait_recv()
        f_copy(d).start()
        if across:
            d_copy(2 - d).start()
    take_k(1, 1)
    split_new(1)
    zs(1, 1, 0, 2)
    for d in near:
        f_copy(d).wait_recv()
    upto = 2 + 2 * len(near)
    xs(2, upto)
    zs(0, 0, 2, upto)
    take_k(2, 0)
    if across:
        for half in range(2):
            d_copy(half).wait_recv()
        f_copy(3).start()
    zs(1, 1, 2, upto)
    take_k(2, 1)
    split_new(2)
    zs(2, 2, 0, upto)
    if across:
        f_copy(3).wait_recv()
        xs(upto, ntm)
        zs(0, 2, upto, ntm)
    def last_side(h, step):
        def side(direction, _):
            b = z + h * (1 - 2 * direction)

            @pl.when((b >= 0) & (b < nop))
            def _():
                step(b)

            return 0

        lax.fori_loop(0, 2, side, 0)

    def by(group, b, work):
        def at(n, _):
            for k in range(group):
                work(b, group * n + k)
            return 0

        lax.fori_loop(0, ntm // group, at, 0)

    for h in range(3, nop):
        if h < nop - 1:
            for chunk in range(len(pieces(h))):
                take_k(h, chunk)
            split_new(h)
            zs(h, h, 0, ntm)
            continue

        def put_piece(b, n):
            k, lo, size = fine[n]
            hi, small = halves(k_buf[b, k, lo:lo + size, :])
            kk_buf[b, k, lo:lo + size, :] = hi
            kk_buf[b, k, order + lo:order + lo + size, :] = small

        def right_of(b, k, lo, size):
            hi, small = kk_buf[b, k, lo:lo + size, :], kk_buf[b, k, order + lo:order + lo + size, :]
            return jnp.concatenate([hi, hi, small], axis=0)

        def left_of(j, x, lo, size):
            hi, small = x_buf[j, x, :, lo:lo + size], x_buf[j, x, :, order + lo:order + lo + size]
            return jnp.concatenate([hi, small, hi], axis=1)

        def dot(left, right):
            return jnp.dot(left, right, preferred_element_type=f32)

        def real_part(b):
            put_piece(b, 0)
            right = right_of(b, 0, 0, order)

            def step(b, j):
                p_buf[j, 0] = dot(left_of(j, 0, 0, order), right)
                p_buf[j, 1] = dot(left_of(j, 1, 0, order), right)

            by(ntm, b, step)

        def upper_part(b):
            put_piece(b, 1)
            right = right_of(b, 1, 0, strip)

            def step(b, j):
                p_buf[j, 0] = p_buf[j, 0] - dot(left_of(j, 1, 0, strip), right)
                p_buf[j, 1] = p_buf[j, 1] + dot(left_of(j, 0, 0, strip), right)

            by(ntm, b, step)

        def last_part(b):
            put_piece(b, 2)
            right = right_of(b, 1, strip, strip)

            def step(b, j):
                z_re = p_buf[j, 0] - dot(left_of(j, 1, strip, strip), right)
                z_im = p_buf[j, 1] + dot(left_of(j, 0, strip, strip), right)
                trace(b, j, z_re, z_im)

            by(ntm, b, step)

        take_k(h, 0)
        last_side(h, real_part)
        take_k(h, 1)
        last_side(h, upper_part)
        take_k(h, 2)
        last_side(h, last_part)

    for copy in lists:
        copy.wait()
    at_row = lax.broadcasted_iota(jnp.int32, (ntm, ntm), 0)
    at_lane = lax.broadcasted_iota(jnp.int32, (ntm, ntm), 1)

    def total(b, part):
        sums = jnp.sum(tr_buf[b, part], axis=1, keepdims=True)
        return jnp.sum(jnp.where(at_row == at_lane, sums, 0.0), axis=0, keepdims=True)

    table = [[total(b, part) for part in range(2)] for b in range(nop)]
    for s in range(slots):
        for part in range(2):
            picked = jnp.zeros((1, ntm), f32)
            for b in range(nop):
                picked = jnp.where(pl_ref[s] == b, table[b][part], picked)
            out_ref[2 * s + part:2 * s + part + 1, :] = jnp.where(s < pc_ref[0], picked, 0.0)

    for d in near:
        s_copy(d).wait_send()
    if across:
        for half in range(2):
            d_copy(half).wait_send()
    for d in range(nq):
        f_copy(d).wait_send()
    for direction in range(2):
        for h in range(1, nop):
            @pl.when(sends(direction, h))
            def _():
                for chunk in range(len(pieces(h))):
                    k_copy(direction, h, chunk, h == 1).wait_send()


def body(ntm, nop, perambs, src_ops, sink_ops, pair_list, pair_count):
    order = perambs.shape[-1]
    slots = pair_list.shape[1]
    times = perambs.shape[1]
    nq = ntm // 2
    block = (2, order, order)
    parts = pl.pallas_call(
        functools.partial(kernel, ntm, nop, slots, order),
        out_shape=pltpu.VMEM((2 * slots, times), f32),
        in_specs=[pl.BlockSpec(memory_space=pl.ANY)] * 5,
        out_specs=pl.BlockSpec(memory_space=pltpu.VMEM),
        scratch_shapes=[
            pltpu.VMEM((times,) + block, f32),
            pltpu.VMEM((2, nq) + block, f32),
            pltpu.VMEM((nop,) + block, f32),
            pltpu.VMEM((times, 3, order, 2 * order), bf16),
            pltpu.VMEM((nop, 3, 2 * order, order), bf16),
            pltpu.VMEM((times, 4, order, 2 * order), bf16),
            pltpu.VMEM((3, order, 2 * order), bf16),
            pltpu.VMEM((3, 2 * order, order), bf16),
            pltpu.VMEM((nop, 2, times, 128), f32),
            pltpu.SMEM((slots,), jnp.int32),
            pltpu.SMEM((1,), jnp.int32),
            pltpu.SemaphoreType.DMA((2,)),
            pltpu.SemaphoreType.DMA((times,)),
            pltpu.SemaphoreType.DMA((2,)),
            pltpu.SemaphoreType.DMA((nq,)),
            pltpu.SemaphoreType.DMA((2, nq)),
            pltpu.SemaphoreType.DMA((nq,)),
            pltpu.SemaphoreType.DMA((2,)),
            pltpu.SemaphoreType.DMA((2,)),
            pltpu.SemaphoreType.DMA((2, nop, 3)),
            pltpu.SemaphoreType.DMA((2, nop, 3)),
        ],
        compiler_params=pltpu.CompilerParams(
            collective_id=0, has_side_effects=True, vmem_limit_bytes=64 * 1000 * 1000),
    )(pair_list[0], pair_count, perambs[0], src_ops[0, 0], sink_ops[0, 0])
    return parts.reshape(1, slots, 1, 2, times)


def solution(mesh):
    placed = (
        P("tm", None, None, None, None),
        P("op", "tm", None, None, None),
        P("op", "tm", None, None, None),
        P("op", None),
        P("op"),
    )
    return jax.shard_map(
        functools.partial(body, mesh.shape["tm"], mesh.shape["op"]),
        mesh=mesh, in_specs=placed, out_specs=P("op", None, "tm", None, None), check_vma=False
    )
```
